32 devices in a mesh: grp: 2 (over x), win: 4 (over z), seq: 4 (over y, core).
Axes of the slice: x: 2, y: 2, z: 4, core: 2. Of those that a mesh axis runs over, the one named last changes fastest.
Arguments:
- embeddings: bfloat16 [8, 768, 1536], P(('grp', 'win'), 'seq'), parts along dimension 0, may hold values from -48 to 48
- skip_rows: bfloat16 [8, 1536, 1536], P(('grp', 'win'), 'seq'), parts along dimension 0, may hold values from -6 to 6
- w_query: bfloat16 [1536, 256], replicated, may hold values from -0.16 to 0.16
- w_key: bfloat16 [1536, 256], replicated, may hold values from -10 to 10
- w_value: bfloat16 [1536, 768], replicated, may hold values from -0.15625 to 0.15625
- w_out: bfloat16 [768, 1536], replicated, may hold values from -0.21875 to 0.21875
- conv_taps: float32 [3, 1536], replicated, may hold values from -3 to 3
- w_head: bfloat16 [1536, 4096], P(None, 'seq'), may hold values from -0.15625 to 0.15625
- head_bias: float32 [4096], replicated, may hold values from -4 to 4
Outputs:
- genome_tracks: bfloat16 [8, 2, 4, 96, 4096], P(('grp', 'win'), None, 'seq'), parts along dimension 0
The draws below stay inside these ranges and needn't reach their ends.
There are 2 independent parts, one for each index of `grp`. The reference program is written for one: setup_inputs(seed, part) draws one part's arguments, and reference() takes and returns one part's arrays. A program takes and returns all parts, laid end to end along the dimension named above; an argument that names none is the same for every part. Nothing has to cross between parts.
All inputs are finite; a program needn't handle non-finite values.
Results may differ from the reference program's by a relative error of at most 0.0075.
Values may be sent and summed in bfloat16 or wider, within the bound.
A program may use at most 128 MiB of HBM per device.

```python
import math
import jax
import jax.numpy as jnp
from jax import lax

D = 1536
HEADS = 4
KEY = 64
VAL = 192
TRACKS = 4096
WIN_LEN = 768
PIECE = 96
N_WIN = 4
N_SEQ = 4


def draw_pair(key):
    limit = min(6.0 / math.sqrt(D), 0.155)
    first = jax.random.normal(jax.random.fold_in(key, 11), (D, HEADS * KEY), jnp.float32) / math.sqrt(D)
    second = jax.random.normal(jax.random.fold_in(key, 12), (D, HEADS * KEY), jnp.float32) / math.sqrt(D)
    first = jnp.clip(first, -limit, limit)
    second = 4.0 * jnp.clip(second, -limit, limit)
    return (first, second)


def draw_w_query(key, part):
    return draw_pair(key)[0].astype(jnp.bfloat16)


def draw_w_key(key, part):
    return draw_pair(key)[1].astype(jnp.bfloat16)


def draw_embeddings(key, part):
    base = jax.random.normal(jax.random.fold_in(key, 21), (N_WIN, WIN_LEN, D), jnp.float32)
    base = jnp.clip(base, -6.0, 6.0)
    return base.astype(jnp.bfloat16)


def steps_of(rng, extent, shards, low, top_value):
    level = 1.0
    for axis_at, blocks in shards:
        steps = jax.random.uniform(jax.random.fold_in(jax.random.fold_in(rng, 6), axis_at), (blocks,), jnp.float32, low / len(shards), top_value / len(shards))
        level = level * jnp.repeat(jnp.exp(steps), extent[axis_at] // blocks).reshape((-1,) + (1,) * (len(extent) - 1 - axis_at))
    return level


def bell_draw(rng, dims, width, reach, pieces=(), kind=jnp.bfloat16):
    values = jax.random.normal(rng, dims, jnp.float32) * width
    if len(pieces) > 0:
        values = steps_of(rng, dims, pieces, -0.22, 0.18) * values
    return jnp.clip(values, min=-reach, max=reach).astype(kind)


def setup_inputs(seed: int = 0, part: int = 0) -> dict:
    key_list = jax.random.split(jax.random.key(seed), 10)
    own_keys = jax.random.split(jax.random.fold_in(key_list[9], part), 10)
    return {
        "embeddings": draw_embeddings(jax.random.fold_in(jax.random.fold_in(key_list[9], part), 71), part),
        "skip_rows": bell_draw(own_keys[1], (N_WIN, 2 * WIN_LEN, D), 1.0, 6.0, ((0, 4), (1, 4))),
        "w_query": draw_w_query(jax.random.fold_in(key_list[9], 71), part),
        "w_key": draw_w_key(jax.random.fold_in(key_list[9], 71), part),
        "w_value": bell_draw(key_list[4], (D, HEADS * VAL), D ** -0.5, 0.15625),
        "w_out": bell_draw(key_list[5], (HEADS * VAL, D), (HEADS * VAL) ** -0.5, 0.21875),
        "conv_taps": bell_draw(key_list[6], (3, D), 0.6, 3.0, (), jnp.float32),
        "w_head": bell_draw(key_list[7], (D, TRACKS), D ** -0.5, 0.15625, ((1, 4),)),
        "head_bias": bell_draw(key_list[8], (TRACKS,), 1.0, 4.0, (), jnp.float32),
    }


def rounded(values):
    return lax.optimization_barrier(values.astype(jnp.bfloat16))

def normalize(rows):
    centre = lax.optimization_barrier(jnp.mean(rows, axis=-1, keepdims=True))
    centred = rows - centre
    spread = lax.optimization_barrier(jnp.mean(centred * centred, axis=-1, keepdims=True))
    return centred * lax.rsqrt(spread + 1e-05)

def reference(embeddings, skip_rows, w_query, w_key, w_value, w_out, conv_taps, w_head, head_bias):

    def window_tracks(pair):
        embed_win, skip_win = pair
        length = embed_win.shape[0]
        x_float = embed_win.astype(jnp.float32)
        normed = normalize(x_float).astype(jnp.bfloat16)
        query = rounded(jnp.dot(normed, w_query, preferred_element_type=jnp.float32)).reshape(length, HEADS, KEY)
        key_rows = rounded(jnp.dot(normed, w_key, preferred_element_type=jnp.float32)).reshape(length, HEADS, KEY)
        value_rows = rounded(jnp.dot(normed, w_value, preferred_element_type=jnp.float32)).reshape(length, HEADS, VAL)
        scores = jnp.einsum('thk,nhk->thn', query.astype(jnp.float32), key_rows.astype(jnp.float32)) / math.sqrt(KEY)
        top_score = lax.optimization_barrier(jnp.max(scores, axis=-1, keepdims=True))
        expo = jnp.exp(scores - top_score)
        denom_sum = lax.optimization_barrier(jnp.sum(expo, axis=-1))
        weights = rounded(expo).astype(jnp.float32)
        attended = jnp.einsum('thn,nhv->thv', weights, value_rows.astype(jnp.float32)) / denom_sum[..., None]
        attended = attended.reshape(length, HEADS * VAL).astype(jnp.bfloat16)
        resid = x_float + jnp.dot(attended, w_out, preferred_element_type=jnp.float32)
        upsampled = rounded(jnp.repeat(resid, 2, axis=0) + skip_win.astype(jnp.float32)).astype(jnp.float32)
        padded = jnp.pad(upsampled, ((1, 1), (0, 0)))
        conv_out = conv_taps[0] * padded[:-2] + conv_taps[1] * padded[1:-1] + conv_taps[2] * padded[2:]
        features = jax.nn.gelu(conv_out, approximate=False).astype(jnp.bfloat16)
        return jnp.dot(features, w_head, preferred_element_type=jnp.float32).astype(jnp.bfloat16)
    tracks = lax.map(window_tracks, (embeddings, skip_rows))
    length = tracks.shape[1] // 2
    ahead_part = tracks[:, :length].astype(jnp.float32)
    behind = jnp.roll(tracks[:, length:], 1, axis=0).astype(jnp.float32)
    offsets = jnp.arange(length, dtype=jnp.int32).astype(jnp.float32)[:, None]
    stitched = ((offsets + 1.0) * ahead_part + (length - offsets) * behind) / (length + 1.0) + head_bias
    genome_tracks = jax.nn.softplus(stitched).astype(jnp.bfloat16)
    return genome_tracks.reshape(N_WIN, N_SEQ // 2, N_SEQ, PIECE, TRACKS)
```

```python
import functools
import math

import jax
import jax.numpy as jnp
from jax import lax
from jax.experimental import pallas as pl
from jax.experimental.pallas import tpu as pltpu
from jax.sharding import PartitionSpec as P

HEADS = 4
KEY = 64
VAL = 192
PAIRS = HEADS // 2
KP = 2 * KEY
VP = 2 * VAL
TILE = 256
HEAD_TILE = 512
EARLY = 3
MIDDLE = 5
MESH = pl.DeviceIdType.MESH


def normalize(rows):
    centre = jnp.mean(rows, axis=-1, keepdims=True)
    centred = rows - centre
    spread = jnp.mean(centred * centred, axis=-1, keepdims=True)
    return centred * lax.rsqrt(spread + 1e-05)


def gelu(x):
    return 0.5 * x * (1.0 + lax.erf(x * math.sqrt(0.5)))


def kernel(
    n, n_win, n_grp,
    emb_h, skip_h, wq_h, wk_h, wv_h, wo_h, taps_h, wh_h, bias_h, out_h,
    x_v, skip_v, wq_v, wk_v, wv_v, wo_v, taps_v, bias_v, wh_v,
    xh_v, sh_v, q_v, kv_v, att_v, wide_v, even_v, odd_v,
    feat_v, mid_v, got_v, blend_v, acc_v, out_v,
    load_sem, send_sem, recv_sem, fsend_sem, frecv_sem, bsend_sem, brecv_sem,
    store_sem, psend_sem, precv_sem,
):
    grp = lax.axis_index("grp")
    win = lax.axis_index("win")
    seq = lax.axis_index("seq")
    tok, width = x_v.shape
    piece = feat_v.shape[1]
    cols = wh_v.shape[2]
    half = n // 2
    bands = width // TILE
    window_len = n * tok
    core = seq % 2
    row = seq // 2

    def dev(g, w, s):
        return (g, w, s)

    sibling = dev(grp, win, seq + 1 - 2 * core)
    other_grp = 1 - grp
    other_win = win + 1 - 2 * (win % 2)
    across = dev(other_grp, win, seq)
    beside = dev(grp, other_win, seq)
    peers = [(seq + 2 * e) % n for e in range(1, half)]
    next_win = (win + 1) % n_win
    prev_win = (win + n_win - 1) % n_win

    barrier = pltpu.get_barrier_semaphore()
    greeted = [dev(grp, win, (seq + d) % n) for d in range(1, n)]
    greeted += [dev(grp, w, seq) for w in (next_win, prev_win)]
    greeted.append(across)
    for target in greeted:
        pl.semaphore_signal(barrier, inc=1, device_id=target, device_id_type=MESH)

    loads = {}
    for at, (name, src, dst) in enumerate(
        (
            ("x", emb_h.at[0], x_v),
            ("wk", wk_h, wk_v),
            ("wv", wv_h, wv_v),
            ("wq", wq_h, wq_v),
            ("skip", skip_h.at[0], skip_v),
            ("wo", wo_h, wo_v),
            ("taps", taps_h, taps_v),
            ("wh", wh_h, wh_v.at[row]),
            ("bias", bias_h, bias_v),
        )
    ):
        loads[name] = pltpu.make_async_copy(src, dst, load_sem.at[at])
        loads[name].start()

    pl.semaphore_wait(barrier, len(greeted))

    started = []

    def remote(src, dst, target):
        at = len(started)
        copy = pltpu.make_async_remote_copy(
            src_ref=src,
            dst_ref=dst,
            send_sem=send_sem.at[at],
            recv_sem=recv_sem.at[at],
            device_id=target,
            device_id_type=MESH,
        )
        copy.start()
        started.append(copy)
        return copy

    chunk = TILE // (2 * n_grp)

    def rows_of(g, w, c):
        return pl.ds(pl.multiple_of(c * TILE + (g * 2 + w % 2) * chunk, chunk), chunk)

    arrived = set()

    def arrive(copy):
        if id(copy) not in arrived:
            arrived.add(id(copy))
            copy.wait_recv()

    far = [(row + half - e) % half for e in range(1, half)]
    y_in, x_in, z_in, diag_in = {}, {}, {}, {}

    def head_out(c):
        rows = rows_of(grp, win, c)
        y_in[c] = [remote(wh_h.at[rows], wh_v.at[row, rows], dev(grp, win, p)) for p in peers]

    def head_spread(c):
        rows = rows_of(grp, win, c)
        x_in[c], z_in[c] = [], []
        for copy, at in zip(y_in[c], far):
            arrive(copy)
            block = wh_v.at[at, rows]
            z_in[c].append(remote(block, block, beside))
            x_in[c].append(remote(block, block, across))

    def head_relay(c):
        diag_in[c] = []
        for copy, at in zip(z_in[c], far):
            arrive(copy)
            block = wh_v.at[at, rows_of(grp, other_win, c)]
            diag_in[c].append(remote(block, block, across))

    def head_ready(c):
        for copies in (y_in, x_in, z_in, diag_in):
            for copy in copies[c]:
                arrive(copy)

    next_seq = dev(grp, win, (seq + 1) % n)
    prev_seq = dev(grp, win, (seq + n - 1) % n)
    edges = [
        remote(emb_h.at[0, pl.ds(tok - 8, 8)], xh_v.at[0], next_seq),
        remote(emb_h.at[0, pl.ds(0, 8)], xh_v.at[1], prev_seq),
        remote(skip_h.at[0, pl.ds(2 * tok - 8, 8)], sh_v.at[0], next_seq),
        remote(skip_h.at[0, pl.ds(0, 8)], sh_v.at[1], prev_seq),
    ]
    for c in range(EARLY):
        head_out(c)

    loads["x"].wait()
    normed = normalize(x_v[...].astype(jnp.float32)).astype(jnp.bfloat16)
    loads["wk"].wait()
    loads["wv"].wait()
    kv_far, kv_near = [], []
    for p in range(PAIRS):
        kv_v[seq, p, :, :KP] = jnp.dot(
            normed, wk_v[:, p * KP : (p + 1) * KP], preferred_element_type=jnp.float32
        ).astype(jnp.bfloat16)
        kv_v[seq, p, :, KP:] = jnp.dot(
            normed, wv_v[:, p * VP : (p + 1) * VP], preferred_element_type=jnp.float32
        ).astype(jnp.bfloat16)
        block = kv_v.at[seq, p]
        kv_far.append([remote(block, block, dev(grp, win, s)) for s in peers])
        kv_near.append([remote(block, block, sibling)])
    for c in range(EARLY, MIDDLE):
        head_out(c)
    loads["wq"].wait()
    q_v[:tok] = jnp.dot(normed, wq_v[...], preferred_element_type=jnp.float32).astype(jnp.bfloat16)
    for copy in edges:
        copy.wait_recv()
    edge_x = jnp.concatenate([xh_v[0].astype(jnp.float32), xh_v[1].astype(jnp.float32)], axis=0)
    q_v[tok:] = jnp.dot(
        normalize(edge_x).astype(jnp.bfloat16), wq_v[...], preferred_element_type=jnp.float32
    ).astype(jnp.bfloat16)
    loads["skip"].wait()
    for j in range(width // 128):
        wide_v[j] = skip_v[:, j * 128 : (j + 1) * 128].astype(jnp.float32)

    def kv_relay(p):
        for e in range(half - 1):
            kv_far[p][e].wait_recv()
            block = kv_v.at[(seq + n - 2 * (e + 1)) % n, p]
            kv_near[p].append(remote(block, block, sibling))

    def attend(p):
        for copy in kv_near[p]:
            copy.wait_recv()
        keys = kv_v[:, p, :, :KP].reshape(n * tok, KP)
        vals = kv_v[:, p, :, KP:].reshape(n * tok, VP)
        pair = q_v[:, p * KP : (p + 1) * KP]
        key_lane = lax.broadcasted_iota(jnp.int32, pair.shape, 1)
        outs = []
        for h in range(2):
            mine = key_lane < KEY if h == 0 else key_lane >= KEY
            masked = jnp.where(mine, pair.astype(jnp.float32), 0.0).astype(jnp.bfloat16)
            scores = lax.dot_general(
                masked, keys, (((1,), (1,)), ((), ())), preferred_element_type=jnp.float32
            ) * (1.0 / math.sqrt(KEY))
            expo = jnp.exp(scores - jnp.max(scores, axis=-1, keepdims=True))
            denom = jnp.sum(expo, axis=-1, keepdims=True)
            outs.append(
                jnp.dot(expo.astype(jnp.bfloat16), vals, preferred_element_type=jnp.float32) / denom
            )
        val_lane = lax.broadcasted_iota(jnp.int32, outs[0].shape, 1)
        att_v[:, p * VP : (p + 1) * VP] = jnp.where(val_lane < VAL, outs[0], outs[1]).astype(
            jnp.bfloat16
        )

    def up_band(b):
        at = slice(b * TILE, (b + 1) * TILE)
        mixed = jnp.dot(att_v[...], wo_v[:, at], preferred_element_type=jnp.float32)
        resid = x_v[:, at].astype(jnp.float32) + mixed[:tok]
        first = xh_v[0, :, at].astype(jnp.float32) + mixed[tok : tok + 8]
        last = xh_v[1, :, at].astype(jnp.float32) + mixed[tok + 8 :]
        first = (first[7:8] + sh_v[0, :, at].astype(jnp.float32)[7:8]).astype(jnp.bfloat16)
        last = (last[0:1] + sh_v[1, :, at].astype(jnp.float32)[0:1]).astype(jnp.bfloat16)
        before = jnp.where(seq == 0, 0.0, first.astype(jnp.float32))
        after = jnp.where(seq == n - 1, 0.0, last.astype(jnp.float32))
        for m in range(TILE // 128):
            j = b * (TILE // 128) + m
            mine = resid[:, m * 128 : (m + 1) * 128]
            even_v[m] = (
                (mine + wide_v[j, pl.ds(0, tok, stride=2), :]).astype(jnp.bfloat16).astype(jnp.float32)
            )
            odd_v[m] = (
                (mine + wide_v[j, pl.ds(1, tok, stride=2), :]).astype(jnp.bfloat16).astype(jnp.float32)
            )
        for m in range(TILE // 128):
            j = b * (TILE // 128) + m
            here = slice(j * 128, (j + 1) * 128)
            lanes = slice(m * 128, (m + 1) * 128)
            even, odd = even_v[m], odd_v[m]
            line = lax.broadcasted_iota(jnp.int32, (tok, 128), 0)
            odd_prev = jnp.where(line == 0, before[:, lanes], pltpu.roll(odd, 1, axis=0))
            even_next = jnp.where(line == tok - 1, after[:, lanes], pltpu.roll(even, tok - 1, axis=0))
            t0, t1, t2 = taps_v[0:1, here], taps_v[1:2, here], taps_v[2:3, here]
            wide_v[j, pl.ds(0, tok, stride=2), :] = gelu(t0 * odd_prev + t1 * even + t2 * odd)
            wide_v[j, pl.ds(1, tok, stride=2), :] = gelu(t0 * even + t1 * odd + t2 * even_next)
            for k in range(n):
                feat_v[k, :, here] = wide_v[j, k * piece : (k + 1) * piece, :].astype(jnp.bfloat16)

    feats = []

    def feature_out(b):
        span = pl.ds(b * TILE, TILE)
        for d in list(range(half, n)) + list(range(1, half)):
            owner = (seq + d) % n
            feats.append(
                pltpu.make_async_remote_copy(
                    src_ref=feat_v.at[owner, :, span],
                    dst_ref=mid_v.at[seq, :, span],
                    send_sem=fsend_sem.at[d, b],
                    recv_sem=frecv_sem.at[seq, b],
                    device_id=dev(grp, win, owner),
                    device_id_type=MESH,
                )
            )
            feats[-1].start()
        mid_v[seq, :, span] = feat_v[seq, :, span]

    def feature_wait(slot, b):
        span = pl.ds(b * TILE, TILE)
        pltpu.make_async_remote_copy(
            src_ref=feat_v.at[slot, :, span],
            dst_ref=mid_v.at[slot, :, span],
            send_sem=fsend_sem.at[0, b],
            recv_sem=frecv_sem.at[slot, b],
            device_id=dev(grp, win, slot),
            device_id_type=MESH,
        ).wait_recv()

    behind = {}

    def feature_forward(b):
        span = pl.ds(b * TILE, TILE)
        behind[b] = []
        for i in range(half):
            at = (seq + i) % half
            if i == 0:

                @pl.when(seq < half)
                def _():
                    feature_wait(half + at, b)

            else:
                feature_wait(half + at, b)
            behind[b].append(
                pltpu.make_async_remote_copy(
                    src_ref=mid_v.at[half + at, :, span],
                    dst_ref=got_v.at[at, :, span],
                    send_sem=bsend_sem.at[i, b],
                    recv_sem=brecv_sem.at[i, b],
                    device_id=dev(grp, next_win, seq),
                    device_id_type=MESH,
                )
            )
            behind[b][i].start()

    paired = {}

    def blend(b):
        for i in range(half):
            at = (seq + i) % half
            if i == 0:

                @pl.when(seq >= half)
                def _():
                    feature_wait(at, b)

            else:
                feature_wait(at, b)
        for copy in behind[b]:
            copy.wait_recv()
        for m in range(TILE // 128):
            at = slice(b * TILE + m * 128, b * TILE + (m + 1) * 128)
            blocks = []
            for i in range(half):
                place = lax.broadcasted_iota(jnp.int32, (piece, 128), 0) + (i * n + seq) * piece
                place = place.astype(jnp.float32)
                blocks.append(
                    (
                        (place + 1.0) * mid_v[i, :, at].astype(jnp.float32)
                        + (window_len - place) * got_v[i, :, at].astype(jnp.float32)
                    )
                    * (1.0 / (window_len + 1.0))
                )
            blend_v[0, :, at] = jnp.concatenate(blocks, axis=0).astype(jnp.bfloat16)
        span = pl.ds(b * TILE, TILE)
        paired[b] = remote(blend_v.at[0, :, span], blend_v.at[1, :, span], sibling)

    step = min(cols, HEAD_TILE)
    steps = cols // step

    def head_product(b, who, h, t):
        at = pl.ds(pl.multiple_of(t * step, step), step)
        span = slice(b * TILE, (b + 1) * TILE)
        return jnp.dot(blend_v[who, :, span], wh_v[h, span, at], preferred_element_type=jnp.float32)

    def head_add(b, who):
        def body(k, carry):
            h, t = k // steps, k % steps
            at = pl.ds(pl.multiple_of(k * step, step), step)
            part = head_product(b, who, h, t)
            acc_v[who, :, at] = part if b == 0 else acc_v[who, :, at] + part
            return carry

        lax.fori_loop(0, half * steps, body, 0)

    stores = []

    def head_last(who):
        b = bands - 1
        for h in range(half):
            shard = 2 * h + core

            def body(t, carry):
                at = pl.ds(pl.multiple_of(h * cols + t * step, step), step)
                base = pl.ds(pl.multiple_of(shard * cols + t * step, step), step)
                z = acc_v[who, :, at] + head_product(b, who, h, t) + bias_v[:, base]
                z = jnp.maximum(z, 0.0) + jnp.log1p(jnp.exp(-jnp.abs(z)))
                for i in range(half):
                    out_v[who, i, :, at] = z[i * piece : (i + 1) * piece].astype(jnp.bfloat16)
                return carry

            lax.fori_loop(0, steps, body, 0)
            src = out_v.at[who, :, :, pl.ds(h * cols, cols)]
            dst = out_h.at[:, :, pl.ds(pl.multiple_of(shard * cols, cols), cols)]
            if who == 0:
                stores.append(pltpu.make_async_copy(src, dst, store_sem.at[h]))
            else:
                stores.append(
                    pltpu.make_async_remote_copy(
                        src_ref=src,
                        dst_ref=dst,
                        send_sem=psend_sem.at[h],
                        recv_sem=precv_sem.at[h],
                        device_id=sibling,
                        device_id_type=MESH,
                    )
                )
            stores[-1].start()

    def head_band(b):
        head_ready(b)
        for who in range(2):
            if who == 1:
                paired[b].wait_recv()
            if b < bands - 1:
                head_add(b, who)
            else:
                head_last(who)

    head_spread(0)
    head_spread(1)
    head_relay(0)
    head_spread(2)
    head_relay(1)
    kv_relay(0)
    head_relay(2)
    attend(0)
    for p in range(1, PAIRS):
        kv_relay(p)
        attend(p)
    loads["wo"].wait()
    loads["taps"].wait()
    for b in range(bands):
        up_band(b)
        feature_out(b)
        if b == 1:
            for c in range(MIDDLE, bands):
                head_out(c)
            head_spread(3)
    loads["wh"].wait()
    loads["bias"].wait()
    head_spread(4)
    head_relay(3)
    feature_forward(0)
    feature_forward(1)
    head_relay(4)
    head_spread(5)
    blend(0)
    feature_forward(2)
    head_band(0)
    blend(1)
    feature_forward(3)
    head_band(1)
    head_relay(5)
    blend(2)
    feature_forward(4)
    head_band(2)
    blend(3)
    feature_forward(5)
    head_band(3)
    blend(4)
    head_band(4)
    blend(5)
    head_band(5)

    for copy in stores:
        copy.wait()
    for copy in started:
        copy.wait_send()
    for copy in feats:
        copy.wait_send()
    for copies in behind.values():
        for copy in copies:
            copy.wait_send()


def local(embeddings, skip_rows, w_query, w_key, w_value, w_out, conv_taps, w_head, head_bias):
    n = lax.axis_size("seq")
    n_win = lax.axis_size("win")
    n_grp = lax.axis_size("grp")
    _, tok, width = embeddings.shape
    cols = w_head.shape[1]
    piece = 2 * tok // n
    half = n // 2
    others = half - 1
    bands = width // TILE
    copies = PAIRS * (2 * others + 1) + 4 * bands * others + bands + 4
    bf16, f32 = jnp.bfloat16, jnp.float32
    dma = pltpu.SemaphoreType.DMA
    tracks = pl.pallas_call(
        functools.partial(kernel, n, n_win, n_grp),
        out_shape=jax.ShapeDtypeStruct((half, piece, n * cols), bf16),
        in_specs=[pl.BlockSpec(memory_space=pl.ANY)] * 9,
        out_specs=pl.BlockSpec(memory_space=pl.ANY),
        scratch_shapes=[
            pltpu.VMEM((tok, width), bf16),
            pltpu.VMEM((2 * tok, width), bf16),
            pltpu.VMEM(w_query.shape, bf16),
            pltpu.VMEM(w_key.shape, bf16),
            pltpu.VMEM(w_value.shape, bf16),
            pltpu.VMEM(w_out.shape, bf16),
            pltpu.VMEM(conv_taps.shape, f32),
            pltpu.VMEM((1, n * cols), f32),
            pltpu.VMEM((half, width, cols), bf16),
            pltpu.VMEM((2, 8, width), bf16),
            pltpu.VMEM((2, 8, width), bf16),
            pltpu.VMEM((tok + 16, HEADS * KEY), bf16),
            pltpu.VMEM((n, PAIRS, tok, KP + VP), bf16),
            pltpu.VMEM((tok + 16, HEADS * VAL), bf16),
            pltpu.VMEM((width // 128, 2 * tok, 128), f32),
            pltpu.VMEM((TILE // 128, tok, 128), f32),
            pltpu.VMEM((TILE // 128, tok, 128), f32),
            pltpu.VMEM((n, piece, width), bf16),
            pltpu.VMEM((n, piece, width), bf16),
            pltpu.VMEM((half, piece, width), bf16),
            pltpu.VMEM((2, tok, width), bf16),
            pltpu.VMEM((2, tok, half * cols), f32),
            pltpu.VMEM((2, half, piece, half * cols), bf16),
            dma((9,)),
            dma((copies,)),
            dma((copies,)),
            dma((n, bands)),
            dma((n, bands)),
            dma((half, bands)),
            dma((half, bands)),
            dma((half,)),
            dma((half,)),
            dma((half,)),
        ],
        compiler_params=pltpu.CompilerParams(
            collective_id=0, has_side_effects=True, vmem_limit_bytes=60 * 1024 * 1024
        ),
    )(
        embeddings, skip_rows, w_query, w_key, w_value, w_out, conv_taps, w_head,
        head_bias.reshape(1, -1),
    )
    return tracks[None, :, None]


def solution(mesh):
    return jax.shard_map(
        local,
        mesh=mesh,
        in_specs=(
            P(("grp", "win"), "seq", None),
            P(("grp", "win"), "seq", None),
            P(),
            P(),
            P(),
            P(),
            P(),
            P(None, "seq"),
            P(),
        ),
        out_specs=P(("grp", "win"), None, "seq", None, None),
        check_vma=False,
    )
```

```python
import functools
import math

import jax
import jax.numpy as jnp
from jax import lax
from jax.experimental import pallas as pl
from jax.experimental.pallas import tpu as pltpu
from jax.sharding import PartitionSpec as P

HEADS = 4
KEY = 64
VAL = 192
PAIRS = HEADS // 2
KP = 2 * KEY
VP = 2 * VAL
BANDS = 6
HEAD_TILE = 512
EARLY = 4
LINE = 4
MESH = pl.DeviceIdType.MESH


def normalize(rows):
    centre = jnp.mean(rows, axis=-1, keepdims=True)
    centred = rows - centre
    spread = jnp.mean(centred * centred, axis=-1, keepdims=True)
    return centred * lax.rsqrt(spread + 1e-05)


def gelu(x):
    return 0.5 * x * (1.0 + lax.erf(x * math.sqrt(0.5)))


def kernel(
    n, n_win, n_grp,
    emb_h, skip_h, wq_h, wk_h, wv_h, wo_h, taps_h, wh_h, bias_h, out_h,
    x_v, skip_v, wq_v, wk_v, wv_v, wo_v, taps_v, bias_v, wh_v,
    xh_v, sh_v, q_v, kv_v, att_v, wide_v, even_v, odd_v,
    feat_v, mid_v, got_v, blend_v, acc_v, out_v,
    load_sem, send_sem, recv_sem, fsend_sem, frecv_sem, bsend_sem, brecv_sem,
    store_sem, psend_sem, precv_sem,
):
    grp = lax.axis_index("grp")
    win = lax.axis_index("win")
    seq = lax.axis_index("seq")
    tok, width = x_v.shape
    piece = feat_v.shape[1]
    cols = wh_v.shape[2]
    half = n // 2
    tile = width // BANDS
    window_len = n * tok
    core = seq % 2
    row = seq // 2

    def dev(g, w, s):
        return (g, w, s)

    sibling = dev(grp, win, seq + 1 - 2 * core)
    other_grp = 1 - grp
    other_win = win + 1 - 2 * (win % 2)
    across = dev(other_grp, win, seq)
    beside = dev(grp, other_win, seq)
    peers = [(seq + 2 * e) % n for e in range(1, half)]
    next_win = (win + 1) % n_win
    prev_win = (win + n_win - 1) % n_win

    barrier = pltpu.get_barrier_semaphore()
    greeted = [dev(grp, win, (seq + d) % n) for d in range(1, n)]
    greeted += [dev(grp, w, seq) for w in (next_win, prev_win)]
    greeted.append(across)
    for target in greeted:
        pl.semaphore_signal(barrier, inc=1, device_id=target, device_id_type=MESH)

    loads = {}
    for at, (name, src, dst) in enumerate(
        (
            ("x", emb_h.at[0], x_v),
            ("wk", wk_h, wk_v),
            ("wv", wv_h, wv_v),
            ("wq", wq_h, wq_v),
            ("skip", skip_h.at[0], skip_v),
            ("wo", wo_h, wo_v),
            ("taps", taps_h, taps_v),
            ("wh", wh_h, wh_v.at[row]),
            ("bias", bias_h, bias_v),
        )
    ):
        loads[name] = pltpu.make_async_copy(src, dst, load_sem.at[at])
        loads[name].start()

    pl.semaphore_wait(barrier, len(greeted))

    started, maybe = [], []

    def remote(src, dst, target):
        at = len(started) + len(maybe)
        copy = pltpu.make_async_remote_copy(
            src_ref=src,
            dst_ref=dst,
            send_sem=send_sem.at[at],
            recv_sem=recv_sem.at[at],
            device_id=target,
            device_id_type=MESH,
        )
        copy.start()
        started.append(copy)
        return copy

    place = win % LINE
    left = dev(grp, prev_win, seq)
    right = dev(grp, next_win, seq)
    def remote_if(cond, src, dst, target):
        at = len(started) + len(maybe)
        copy = pltpu.make_async_remote_copy(
            src_ref=src,
            dst_ref=dst,
            send_sem=send_sem.at[at],
            recv_sem=recv_sem.at[at],
            device_id=target,
            device_id_type=MESH,
        )

        @pl.when(cond)
        def _():
            copy.start()

        maybe.append((cond, copy))
        return copy

    def rows_of(g, w, c):
        if c < EARLY:
            part = tile // (LINE * n_grp)
            first = c * tile + (g * LINE + w % LINE) * part
        else:
            part = tile // (2 * n_grp)
            first = c * tile + (g * 2 + w % 2) * part
        return pl.ds(pl.multiple_of(first, part), part)

    arrived = set()

    def arrive(copy):
        if id(copy) not in arrived:
            arrived.add(id(copy))
            copy.wait_recv()

    far = [(row + half - e) % half for e in range(1, half)]
    y_in, x_in, z_in, diag_in = {}, {}, {}, {}

    def head_out(c):
        rows = rows_of(grp, win, c)
        y_in[c] = [remote(wh_h.at[rows], wh_v.at[row, rows], dev(grp, win, p)) for p in peers]

    moving, crossing = {}, {}

    def line_own(c):
        rows = rows_of(grp, win, c)
        x_in[c], moving[c], crossing[c] = [], {}, []
        for e, at in enumerate(far):
            arrive(y_in[c][e])
            block = wh_v.at[at, rows]
            moving[c][1, e, 0] = remote_if(place < LINE - 1, block, block, right)
            moving[c][1, e, 1] = remote_if(place > 0, block, block, left)
            x_in[c].append(remote(block, block, across))

    def line_step(c, s):
        for e, at in enumerate(far):
            for way in range(2):
                has = place >= s if way == 0 else place + s < LINE
                goes = place < LINE - 1 if way == 0 else place > 0
                came = moving[c][s, e, way]

                @pl.when(has)
                def _():
                    came.wait_recv()

                rows = rows_of(grp, place - s if way == 0 else place + s, c)
                block = wh_v.at[at, rows]
                if s < LINE - 1:
                    moving[c][s + 1, e, way] = remote_if(
                        jnp.logical_and(has, goes), block, block, right if way == 0 else left
                    )
                crossing[c].append((has, remote_if(has, block, block, across)))

    def head_spread(c):
        rows = rows_of(grp, win, c)
        x_in[c], z_in[c] = [], []
        for copy, at in zip(y_in[c], far):
            arrive(copy)
            block = wh_v.at[at, rows]
            z_in[c].append(remote(block, block, beside))
            x_in[c].append(remote(block, block, across))

    def head_relay(c):
        diag_in[c] = []
        for copy, at in zip(z_in[c], far):
            arrive(copy)
            block = wh_v.at[at, rows_of(grp, other_win, c)]
            diag_in[c].append(remote(block, block, across))

    def head_ready(c):
        if c < EARLY:
            for copy in x_in[c]:
                arrive(copy)
            for has, copy in crossing[c]:

                @pl.when(has)
                def _():
                    copy.wait_recv()

        else:
            for copies in (y_in, x_in, z_in, diag_in):
                for copy in copies[c]:
                    arrive(copy)

    next_seq = dev(grp, win, (seq + 1) % n)
    prev_seq = dev(grp, win, (seq + n - 1) % n)
    edges = [
        remote(emb_h.at[0, pl.ds(tok - 8, 8)], xh_v.at[0], next_seq),
        remote(emb_h.at[0, pl.ds(0, 8)], xh_v.at[1], prev_seq),
        remote(skip_h.at[0, pl.ds(2 * tok - 8, 8)], sh_v.at[0], next_seq),
        remote(skip_h.at[0, pl.ds(0, 8)], sh_v.at[1], prev_seq),
    ]
    for c in range(EARLY):
        head_out(c)

    loads["x"].wait()
    normed = normalize(x_v[...].astype(jnp.float32)).astype(jnp.bfloat16)
    loads["wk"].wait()
    loads["wv"].wait()
    kv_far, kv_near = [], []
    for p in range(PAIRS):
        kv_v[seq, p, :, :KP] = jnp.dot(
            normed, wk_v[:, p * KP : (p + 1) * KP], preferred_element_type=jnp.float32
        ).astype(jnp.bfloat16)
        kv_v[seq, p, :, KP:] = jnp.dot(
            normed, wv_v[:, p * VP : (p + 1) * VP], preferred_element_type=jnp.float32
        ).astype(jnp.bfloat16)
        block = kv_v.at[seq, p]
        kv_far.append([remote(block, block, dev(grp, win, s)) for s in peers])
        kv_near.append([remote(block, block, sibling)])
    for c in range(EARLY, BANDS):
        head_out(c)
    loads["wq"].wait()
    q_v[:tok] = jnp.dot(normed, wq_v[...], preferred_element_type=jnp.float32).astype(jnp.bfloat16)
    for copy in edges:
        copy.wait_recv()
    edge_x = jnp.concatenate([xh_v[0].astype(jnp.float32), xh_v[1].astype(jnp.float32)], axis=0)
    q_v[tok:] = jnp.dot(
        normalize(edge_x).astype(jnp.bfloat16), wq_v[...], preferred_element_type=jnp.float32
    ).astype(jnp.bfloat16)
    loads["skip"].wait()
    for j in range(width // 128):
        wide_v[j] = skip_v[:, j * 128 : (j + 1) * 128].astype(jnp.float32)

    def kv_relay(p):
        for e in range(half - 1):
            kv_far[p][e].wait_recv()
            block = kv_v.at[(seq + n - 2 * (e + 1)) % n, p]
            kv_near[p].append(remote(block, block, sibling))

    def attend(p):
        for copy in kv_near[p]:
            copy.wait_recv()
        keys = kv_v[:, p, :, :KP].reshape(n * tok, KP)
        vals = kv_v[:, p, :, KP:].reshape(n * tok, VP)
        pair = q_v[:, p * KP : (p + 1) * KP]
        key_lane = lax.broadcasted_iota(jnp.int32, pair.shape, 1)
        outs = []
        for h in range(2):
            mine = key_lane < KEY if h == 0 else key_lane >= KEY
            masked = jnp.where(mine, pair.astype(jnp.float32), 0.0).astype(jnp.bfloat16)
            scores = lax.dot_general(
                masked, keys, (((1,), (1,)), ((), ())), preferred_element_type=jnp.float32
            ) * (1.0 / math.sqrt(KEY))
            expo = jnp.exp(scores - jnp.max(scores, axis=-1, keepdims=True))
            denom = jnp.sum(expo, axis=-1, keepdims=True)
            outs.append(
                jnp.dot(expo.astype(jnp.bfloat16), vals, preferred_element_type=jnp.float32) / denom
            )
        val_lane = lax.broadcasted_iota(jnp.int32, outs[0].shape, 1)
        att_v[:, p * VP : (p + 1) * VP] = jnp.where(val_lane < VAL, outs[0], outs[1]).astype(
            jnp.bfloat16
        )

    def up_band(b):
        at = slice(b * tile, (b + 1) * tile)
        mixed = jnp.dot(att_v[...], wo_v[:, at], preferred_element_type=jnp.float32)
        resid = x_v[:, at].astype(jnp.float32) + mixed[:tok]
        first = xh_v[0, :, at].astype(jnp.float32) + mixed[tok : tok + 8]
        last = xh_v[1, :, at].astype(jnp.float32) + mixed[tok + 8 :]
        first = (first[7:8] + sh_v[0, :, at].astype(jnp.float32)[7:8]).astype(jnp.bfloat16)
        last = (last[0:1] + sh_v[1, :, at].astype(jnp.float32)[0:1]).astype(jnp.bfloat16)
        before = jnp.where(seq == 0, 0.0, first.astype(jnp.float32))
        after = jnp.where(seq == n - 1, 0.0, last.astype(jnp.float32))
        for m in range(tile // 128):
            j = b * (tile // 128) + m
            mine = resid[:, m * 128 : (m + 1) * 128]
            even_v[m] = (
                (mine + wide_v[j, pl.ds(0, tok, stride=2), :]).astype(jnp.bfloat16).astype(jnp.float32)
            )
            odd_v[m] = (
                (mine + wide_v[j, pl.ds(1, tok, stride=2), :]).astype(jnp.bfloat16).astype(jnp.float32)
            )
        for m in range(tile // 128):
            j = b * (tile // 128) + m
            here = slice(j * 128, (j + 1) * 128)
            lanes = slice(m * 128, (m + 1) * 128)
            even, odd = even_v[m], odd_v[m]
            line = lax.broadcasted_iota(jnp.int32, (tok, 128), 0)
            odd_prev = jnp.where(line == 0, before[:, lanes], pltpu.roll(odd, 1, axis=0))
            even_next = jnp.where(line == tok - 1, after[:, lanes], pltpu.roll(even, tok - 1, axis=0))
            t0, t1, t2 = taps_v[0:1, here], taps_v[1:2, here], taps_v[2:3, here]
            wide_v[j, pl.ds(0, tok, stride=2), :] = gelu(t0 * odd_prev + t1 * even + t2 * odd)
            wide_v[j, pl.ds(1, tok, stride=2), :] = gelu(t0 * even + t1 * odd + t2 * even_next)
            for k in range(n):
                feat_v[k, :, here] = wide_v[j, k * piece : (k + 1) * piece, :].astype(jnp.bfloat16)

    feats = []

    def feature_out(b):
        span = pl.ds(b * tile, tile)
        for d in list(range(half, n)) + list(range(1, half)):
            owner = (seq + d) % n
            feats.append(
                pltpu.make_async_remote_copy(
                    src_ref=feat_v.at[owner, :, span],
                    dst_ref=mid_v.at[seq, :, span],
                    send_sem=fsend_sem.at[d, b],
                    recv_sem=frecv_sem.at[seq, b],
                    device_id=dev(grp, win, owner),
                    device_id_type=MESH,
                )
            )
            feats[-1].start()
        mid_v[seq, :, span] = feat_v[seq, :, span]

    def feature_wait(slot, b):
        span = pl.ds(b * tile, tile)
        pltpu.make_async_remote_copy(
            src_ref=feat_v.at[slot, :, span],
            dst_ref=mid_v.at[slot, :, span],
            send_sem=fsend_sem.at[0, b],
            recv_sem=frecv_sem.at[slot, b],
            device_id=dev(grp, win, slot),
            device_id_type=MESH,
        ).wait_recv()

    behind = {}

    def feature_forward(b):
        span = pl.ds(b * tile, tile)
        behind[b] = []
        for i in range(half):
            at = (seq + i) % half
            if i == 0:

                @pl.when(seq < half)
                def _():
                    feature_wait(half + at, b)

            else:
                feature_wait(half + at, b)
            behind[b].append(
                pltpu.make_async_remote_copy(
                    src_ref=mid_v.at[half + at, :, span],
                    dst_ref=got_v.at[at, :, span],
                    send_sem=bsend_sem.at[i, b],
                    recv_sem=brecv_sem.at[i, b],
                    device_id=dev(grp, next_win, seq),
                    device_id_type=MESH,
                )
            )
            behind[b][i].start()

    paired = {}

    def blend(b):
        for i in range(half):
            at = (seq + i) % half
            if i == 0:

                @pl.when(seq >= half)
                def _():
                    feature_wait(at, b)

            else:
                feature_wait(at, b)
        for copy in behind[b]:
            copy.wait_recv()
        for m in range(tile // 128):
            at = slice(b * tile + m * 128, b * tile + (m + 1) * 128)
            blocks = []
            for i in range(half):
                offset = lax.broadcasted_iota(jnp.int32, (piece, 128), 0) + (i * n + seq) * piece
                offset = offset.astype(jnp.float32)
                blocks.append(
                    (
                        (offset + 1.0) * mid_v[i, :, at].astype(jnp.float32)
                        + (window_len - offset) * got_v[i, :, at].astype(jnp.float32)
                    )
                    * (1.0 / (window_len + 1.0))
                )
            blend_v[0, :, at] = jnp.concatenate(blocks, axis=0).astype(jnp.bfloat16)
        span = pl.ds(b * tile, tile)
        paired[b] = remote(blend_v.at[0, :, span], blend_v.at[1, :, span], sibling)

    step = min(cols, HEAD_TILE)
    steps = cols // step

    def head_product(lo, hi, who, h, t):
        at = pl.ds(pl.multiple_of(t * step, step), step)
        span = slice(lo * tile, hi * tile)
        return jnp.dot(blend_v[who, :, span], wh_v[h, span, at], preferred_element_type=jnp.float32)

    def head_add(lo, hi, who):
        for b in range(lo, hi):
            if who == 0:
                head_ready(b)
            else:
                paired[b].wait_recv()

        def body(k, carry):
            h, t = k // steps, k % steps
            at = pl.ds(pl.multiple_of(k * step, step), step)
            part = head_product(lo, hi, who, h, t)
            acc_v[who, :, at] = part if lo == 0 else acc_v[who, :, at] + part
            return carry

        lax.fori_loop(0, half * steps, body, 0)

    stores = []

    def head_last(lo, who, h):
        shard = 2 * h + core
        for t in range(steps):
            at = pl.ds(h * cols + t * step, step)
            base = pl.ds(pl.multiple_of(shard * cols + t * step, step), step)
            z = acc_v[who, :, at] + head_product(lo, BANDS, who, h, t) + bias_v[:, base]
            z = jnp.maximum(z, 0.0) + jnp.log1p(jnp.exp(-jnp.abs(z)))
            for i in range(half):
                out_v[who, i, :, at] = z[i * piece : (i + 1) * piece].astype(jnp.bfloat16)
            src = out_v.at[who, :, :, at]
            dst = out_h.at[:, :, base]
            if who == 0:
                stores.append(pltpu.make_async_copy(src, dst, store_sem.at[h, t]))
            else:
                stores.append(
                    pltpu.make_async_remote_copy(
                        src_ref=src,
                        dst_ref=dst,
                        send_sem=psend_sem.at[h, t],
                        recv_sem=precv_sem.at[h, t],
                        device_id=sibling,
                        device_id_type=MESH,
                    )
                )
            stores[-1].start()

    for c in range(EARLY):
        line_own(c)
    for c in range(EARLY):
        line_step(c, 1)
    kv_relay(0)
    line_step(0, 2)
    attend(0)
    for c in range(1, EARLY):
        line_step(c, 2)
    for p in range(1, PAIRS):
        kv_relay(p)
        attend(p)
    loads["wo"].wait()
    loads["taps"].wait()
    line_step(0, 3)
    up_band(0)
    feature_out(0)
    head_spread(4)
    line_step(1, 3)
    up_band(1)
    feature_out(1)
    line_step(2, 3)
    up_band(2)
    feature_out(2)
    line_step(3, 3)
    up_band(3)
    feature_out(3)
    head_spread(5)
    up_band(4)
    feature_out(4)
    up_band(5)
    feature_out(5)
    loads["wh"].wait()
    loads["bias"].wait()
    feature_forward(0)
    head_relay(4)
    feature_forward(1)
    head_relay(5)
    feature_forward(2)
    feature_forward(3)
    blend(0)
    feature_forward(4)
    blend(1)
    feature_forward(5)
    blend(2)
    head_add(0, 3, 0)
    head_add(0, 3, 1)
    blend(3)
    blend(4)
    blend(5)
    for b in range(3, BANDS):
        head_ready(b)
    head_last(3, 0, 0)
    for b in range(3, BANDS):
        paired[b].wait_recv()
    for h in range(half):
        head_last(3, 1, h)
    for h in range(1, half):
        head_last(3, 0, h)

    for copy in stores:
        copy.wait()
    for copy in started:
        copy.wait_send()
    for cond, copy in maybe:

        @pl.when(cond)
        def _():
            copy.wait_send()

    for copy in feats:
        copy.wait_send()
    for copies in behind.values():
        for copy in copies:
            copy.wait_send()


def local(embeddings, skip_rows, w_query, w_key, w_value, w_out, conv_taps, w_head, head_bias):
    n = lax.axis_size("seq")
    n_win = lax.axis_size("win")
    n_grp = lax.axis_size("grp")
    _, tok, width = embeddings.shape
    cols = w_head.shape[1]
    piece = 2 * tok // n
    half = n // 2
    others = half - 1
    steps = cols // min(cols, HEAD_TILE)
    line = EARLY * (4 + 4 * (LINE - 1) - 2) + (BANDS - EARLY) * 4
    copies = PAIRS * (2 * others + 1) + line * others + BANDS + 4
    bf16, f32 = jnp.bfloat16, jnp.float32
    dma = pltpu.SemaphoreType.DMA
    tracks = pl.pallas_call(
        functools.partial(kernel, n, n_win, n_grp),
        out_shape=jax.ShapeDtypeStruct((half, piece, n * cols), bf16),
        in_specs=[pl.BlockSpec(memory_space=pl.ANY)] * 9,
        out_specs=pl.BlockSpec(memory_space=pl.ANY),
        scratch_shapes=[
            pltpu.VMEM((tok, width), bf16),
            pltpu.VMEM((2 * tok, width), bf16),
            pltpu.VMEM(w_query.shape, bf16),
            pltpu.VMEM(w_key.shape, bf16),
            pltpu.VMEM(w_value.shape, bf16),
            pltpu.VMEM(w_out.shape, bf16),
            pltpu.VMEM(conv_taps.shape, f32),
            pltpu.VMEM((1, n * cols), f32),
            pltpu.VMEM((half, width, cols), bf16),
            pltpu.VMEM((2, 8, width), bf16),
            pltpu.VMEM((2, 8, width), bf16),
            pltpu.VMEM((tok + 16, HEADS * KEY), bf16),
            pltpu.VMEM((n, PAIRS, tok, KP + VP), bf16),
            pltpu.VMEM((tok + 16, HEADS * VAL), bf16),
            pltpu.VMEM((width // 128, 2 * tok, 128), f32),
            pltpu.VMEM((width // BANDS // 128, tok, 128), f32),
            pltpu.VMEM((width // BANDS // 128, tok, 128), f32),
            pltpu.VMEM((n, piece, width), bf16),
            pltpu.VMEM((n, piece, width), bf16),
            pltpu.VMEM((half, piece, width), bf16),
            pltpu.VMEM((2, tok, width), bf16),
            pltpu.VMEM((2, tok, half * cols), f32),
            pltpu.VMEM((2, half, piece, half * cols), bf16),
            dma((9,)),
            dma((copies,)),
            dma((copies,)),
            dma((n, BANDS)),
            dma((n, BANDS)),
            dma((half, BANDS)),
            dma((half, BANDS)),
            dma((half, steps)),
            dma((half, steps)),
            dma((half, steps)),
        ],
        compiler_params=pltpu.CompilerParams(
            collective_id=0, has_side_effects=True, vmem_limit_bytes=60 * 1024 * 1024
        ),
    )(
        embeddings, skip_rows, w_query, w_key, w_value, w_out, conv_taps, w_head,
        head_bias.reshape(1, -1),
    )
    return tracks[None, :, None]


def solution(mesh):
    return jax.shard_map(
        local,
        mesh=mesh,
        in_specs=(
            P(("grp", "win"), "seq", None),
            P(("grp", "win"), "seq", None),
            P(),
            P(),
            P(),
            P(),
            P(),
            P(None, "seq"),
            P(),
        ),
        out_specs=P(("grp", "win"), None, "seq", None, None),
        check_vma=False,
    )
```

```python
import functools
import math

import jax
import jax.numpy as jnp
from jax import lax
from jax.experimental import pallas as pl
from jax.experimental.pallas import tpu as pltpu
from jax.sharding import PartitionSpec as P

HEADS = 4
KEY = 64
VAL = 192
PAIRS = HEADS // 2
KP = 2 * KEY
VP = 2 * VAL
BANDS = 6
HEAD_TILE = 512
EARLY = 4
LINE = 4
MESH = pl.DeviceIdType.MESH


def normalize(rows):
    centre = jnp.mean(rows, axis=-1, keepdims=True)
    centred = rows - centre
    spread = jnp.mean(centred * centred, axis=-1, keepdims=True)
    return centred * lax.rsqrt(spread + 1e-05)


def gelu(x):
    return 0.5 * x * (1.0 + lax.erf(x * math.sqrt(0.5)))


def kernel(
    n, n_win, n_grp,
    emb_h, skip_h, wq_h, wk_h, wv_h, wo_h, taps_h, wh_h, bias_h, out_h,
    x_v, skip_v, wq_v, wk_v, wv_v, wo_v, taps_v, bias_v, wh_v,
    xh_v, sh_v, q_v, kv_v, att_v, wide_v, even_v, odd_v,
    feat_v, mid_v, got_v, blend_v, acc_v, out_v,
    load_sem, send_sem, recv_sem, fsend_sem, frecv_sem, bsend_sem, brecv_sem,
    store_sem, psend_sem, precv_sem,
):
    grp = lax.axis_index("grp")
    win = lax.axis_index("win")
    seq = lax.axis_index("seq")
    tok, width = x_v.shape
    piece = feat_v.shape[1]
    cols = wh_v.shape[2]
    half = n // 2
    tile = width // BANDS
    window_len = n * tok
    core = seq % 2
    row = seq // 2

    def dev(g, w, s):
        return (g, w, s)

    sibling = dev(grp, win, seq + 1 - 2 * core)
    other_grp = 1 - grp
    other_win = win + 1 - 2 * (win % 2)
    across = dev(other_grp, win, seq)
    beside = dev(grp, other_win, seq)
    peers = [(seq + 2 * e) % n for e in range(1, half)]
    next_win = (win + 1) % n_win
    prev_win = (win + n_win - 1) % n_win

    barrier = pltpu.get_barrier_semaphore()
    greeted = [dev(grp, win, (seq + d) % n) for d in range(1, n)]
    greeted += [dev(grp, w, seq) for w in (next_win, prev_win)]
    greeted.append(across)
    for target in greeted:
        pl.semaphore_signal(barrier, inc=1, device_id=target, device_id_type=MESH)

    loads = {}
    local_copies = {
        "x": (emb_h.at[0], x_v),
        "wk": (wk_h, wk_v),
        "wv": (wv_h, wv_v),
        "wq": (wq_h, wq_v),
        "skip": (skip_h.at[0], skip_v),
        "wo": (wo_h, wo_v),
        "taps": (taps_h, taps_v),
        "bias": (bias_h, bias_v),
        "wh": (wh_h, wh_v.at[row]),
    }

    def load(*names):
        for name in names:
            loads[name] = pltpu.make_async_copy(*local_copies[name], load_sem.at[len(loads)])
            loads[name].start()

    load("x", "wk", "wv")
    pl.semaphore_wait(barrier, len(greeted))

    started, maybe = [], []

    def remote(src, dst, target):
        at = len(started) + len(maybe)
        copy = pltpu.make_async_remote_copy(
            src_ref=src,
            dst_ref=dst,
            send_sem=send_sem.at[at],
            recv_sem=recv_sem.at[at],
            device_id=target,
            device_id_type=MESH,
        )
        copy.start()
        started.append(copy)
        return copy

    place = win % LINE
    left = dev(grp, prev_win, seq)
    right = dev(grp, next_win, seq)
    def remote_if(cond, src, dst, target):
        at = len(started) + len(maybe)
        copy = pltpu.make_async_remote_copy(
            src_ref=src,
            dst_ref=dst,
            send_sem=send_sem.at[at],
            recv_sem=recv_sem.at[at],
            device_id=target,
            device_id_type=MESH,
        )

        @pl.when(cond)
        def _():
            copy.start()

        maybe.append((cond, copy))
        return copy

    def rows_of(g, w, c):
        if c < EARLY:
            part = tile // (LINE * n_grp)
            first = c * tile + (g * LINE + w % LINE) * part
        else:
            part = tile // (2 * n_grp)
            first = c * tile + (g * 2 + w % 2) * part
        return pl.ds(pl.multiple_of(first, part), part)

    arrived = set()

    def arrive(copy):
        if id(copy) not in arrived:
            arrived.add(id(copy))
            copy.wait_recv()

    far = [(row + half - e) % half for e in range(1, half)]
    y_in, x_in, z_in, diag_in = {}, {}, {}, {}

    def head_out(c):
        rows = rows_of(grp, win, c)
        y_in[c] = [remote(wh_h.at[rows], wh_v.at[row, rows], dev(grp, win, p)) for p in peers]

    moving, crossing = {}, {}

    def line_own(c):
        rows = rows_of(grp, win, c)
        x_in[c], moving[c], crossing[c] = [], {}, []
        for e, at in enumerate(far):
            arrive(y_in[c][e])
            block = wh_v.at[at, rows]
            moving[c][1, e, 0] = remote_if(place < LINE - 1, block, block, right)
            moving[c][1, e, 1] = remote_if(place > 0, block, block, left)
            x_in[c].append(remote(block, block, across))

    def line_step(c, s):
        for e, at in enumerate(far):
            for way in range(2):
                has = place >= s if way == 0 else place + s < LINE
                goes = place < LINE - 1 if way == 0 else place > 0
                came = moving[c][s, e, way]

                @pl.when(has)
                def _():
                    came.wait_recv()

                rows = rows_of(grp, place - s if way == 0 else place + s, c)
                block = wh_v.at[at, rows]
                if s < LINE - 1:
                    moving[c][s + 1, e, way] = remote_if(
                        jnp.logical_and(has, goes), block, block, right if way == 0 else left
                    )
                crossing[c].append((has, remote_if(has, block, block, across)))

    def head_spread(c):
        rows = rows_of(grp, win, c)
        x_in[c], z_in[c] = [], []
        for copy, at in zip(y_in[c], far):
            arrive(copy)
            block = wh_v.at[at, rows]
            z_in[c].append(remote(block, block, beside))
            x_in[c].append(remote(block, block, across))

    def head_relay(c):
        diag_in[c] = []
        for copy, at in zip(z_in[c], far):
            arrive(copy)
            block = wh_v.at[at, rows_of(grp, other_win, c)]
            diag_in[c].append(remote(block, block, across))

    def head_ready(c):
        if c < EARLY:
            for copy in x_in[c]:
                arrive(copy)
            for has, copy in crossing[c]:

                @pl.when(has)
                def _():
                    copy.wait_recv()

        else:
            for copies in (y_in, x_in, z_in, diag_in):
                for copy in copies[c]:
                    arrive(copy)

    next_seq = dev(grp, win, (seq + 1) % n)
    prev_seq = dev(grp, win, (seq + n - 1) % n)
    for c in range(EARLY):
        head_out(c)
    load("wq")

    loads["x"].wait()
    normed = normalize(x_v[...].astype(jnp.float32)).astype(jnp.bfloat16)
    loads["wk"].wait()
    loads["wv"].wait()
    kv_far, kv_near = [], []
    for p in range(PAIRS):
        kv_v[seq, p, :, :KP] = jnp.dot(
            normed, wk_v[:, p * KP : (p + 1) * KP], preferred_element_type=jnp.float32
        ).astype(jnp.bfloat16)
        kv_v[seq, p, :, KP:] = jnp.dot(
            normed, wv_v[:, p * VP : (p + 1) * VP], preferred_element_type=jnp.float32
        ).astype(jnp.bfloat16)
        block = kv_v.at[seq, p]
        kv_far.append([remote(block, block, dev(grp, win, s)) for s in peers])
        kv_near.append([remote(block, block, sibling)])
    edges = [
        remote(emb_h.at[0, pl.ds(tok - 8, 8)], xh_v.at[0], next_seq),
        remote(emb_h.at[0, pl.ds(0, 8)], xh_v.at[1], prev_seq),
        remote(skip_h.at[0, pl.ds(2 * tok - 8, 8)], sh_v.at[0], next_seq),
        remote(skip_h.at[0, pl.ds(0, 8)], sh_v.at[1], prev_seq),
    ]
    for c in range(EARLY, BANDS):
        head_out(c)
    load("skip", "wo", "taps", "bias", "wh")
    loads["wq"].wait()
    q_v[:tok] = jnp.dot(normed, wq_v[...], preferred_element_type=jnp.float32).astype(jnp.bfloat16)
    def edge_queries():
        for copy in edges:
            copy.wait_recv()
        edge_x = jnp.concatenate([xh_v[0].astype(jnp.float32), xh_v[1].astype(jnp.float32)], axis=0)
        q_v[tok:] = jnp.dot(
            normalize(edge_x).astype(jnp.bfloat16), wq_v[...], preferred_element_type=jnp.float32
        ).astype(jnp.bfloat16)

    def widen():
        loads["skip"].wait()
        for j in range(width // 128):
            wide_v[j] = skip_v[:, j * 128 : (j + 1) * 128].astype(jnp.float32)

    def kv_relay(p):
        for e in range(half - 1):
            kv_far[p][e].wait_recv()
            block = kv_v.at[(seq + n - 2 * (e + 1)) % n, p]
            kv_near[p].append(remote(block, block, sibling))

    def attend(p):
        for copy in kv_near[p]:
            copy.wait_recv()
        keys = kv_v[:, p, :, :KP].reshape(n * tok, KP)
        vals = kv_v[:, p, :, KP:].reshape(n * tok, VP)
        pair = q_v[:, p * KP : (p + 1) * KP]
        key_lane = lax.broadcasted_iota(jnp.int32, pair.shape, 1)
        outs = []
        for h in range(2):
            mine = key_lane < KEY if h == 0 else key_lane >= KEY
            masked = jnp.where(mine, pair.astype(jnp.float32), 0.0).astype(jnp.bfloat16)
            scores = lax.dot_general(
                masked, keys, (((1,), (1,)), ((), ())), preferred_element_type=jnp.float32
            ) * (1.0 / math.sqrt(KEY))
            expo = jnp.exp(scores - jnp.max(scores, axis=-1, keepdims=True))
            denom = jnp.sum(expo, axis=-1, keepdims=True)
            outs.append(
                jnp.dot(expo.astype(jnp.bfloat16), vals, preferred_element_type=jnp.float32) / denom
            )
        val_lane = lax.broadcasted_iota(jnp.int32, outs[0].shape, 1)
        att_v[:, p * VP : (p + 1) * VP] = jnp.where(val_lane < VAL, outs[0], outs[1]).astype(
            jnp.bfloat16
        )

    def up_band(b):
        at = slice(b * tile, (b + 1) * tile)
        mixed = jnp.dot(att_v[...], wo_v[:, at], preferred_element_type=jnp.float32)
        resid = x_v[:, at].astype(jnp.float32) + mixed[:tok]
        first = xh_v[0, :, at].astype(jnp.float32) + mixed[tok : tok + 8]
        last = xh_v[1, :, at].astype(jnp.float32) + mixed[tok + 8 :]
        first = (first[7:8] + sh_v[0, :, at].astype(jnp.float32)[7:8]).astype(jnp.bfloat16)
        last = (last[0:1] + sh_v[1, :, at].astype(jnp.float32)[0:1]).astype(jnp.bfloat16)
        before = jnp.where(seq == 0, 0.0, first.astype(jnp.float32))
        after = jnp.where(seq == n - 1, 0.0, last.astype(jnp.float32))
        for m in range(tile // 128):
            j = b * (tile // 128) + m
            mine = resid[:, m * 128 : (m + 1) * 128]
            even_v[m] = (
                (mine + wide_v[j, pl.ds(0, tok, stride=2), :]).astype(jnp.bfloat16).astype(jnp.float32)
            )
            odd_v[m] = (
                (mine + wide_v[j, pl.ds(1, tok, stride=2), :]).astype(jnp.bfloat16).astype(jnp.float32)
            )
        for m in range(tile // 128):
            j = b * (tile // 128) + m
            here = slice(j * 128, (j + 1) * 128)
            lanes = slice(m * 128, (m + 1) * 128)
            even, odd = even_v[m], odd_v[m]
            line = lax.broadcasted_iota(jnp.int32, (tok, 128), 0)
            odd_prev = jnp.where(line == 0, before[:, lanes], pltpu.roll(odd, 1, axis=0))
            even_next = jnp.where(line == tok - 1, after[:, lanes], pltpu.roll(even, tok - 1, axis=0))
            t0, t1, t2 = taps_v[0:1, here], taps_v[1:2, here], taps_v[2:3, here]
            wide_v[j, pl.ds(0, tok, stride=2), :] = gelu(t0 * odd_prev + t1 * even + t2 * odd)
            wide_v[j, pl.ds(1, tok, stride=2), :] = gelu(t0 * even + t1 * odd + t2 * even_next)
            for k in range(n):
                feat_v[k, :, here] = wide_v[j, k * piece : (k + 1) * piece, :].astype(jnp.bfloat16)

    feats = []

    def feature_out(b):
        span = pl.ds(b * tile, tile)
        for d in list(range(half, n)) + list(range(1, half)):
            owner = (seq + d) % n
            feats.append(
                pltpu.make_async_remote_copy(
                    src_ref=feat_v.at[owner, :, span],
                    dst_ref=mid_v.at[seq, :, span],
                    send_sem=fsend_sem.at[d, b],
                    recv_sem=frecv_sem.at[seq, b],
                    device_id=dev(grp, win, owner),
                    device_id_type=MESH,
                )
            )
            feats[-1].start()
        mid_v[seq, :, span] = feat_v[seq, :, span]

    def feature_wait(slot, b):
        span = pl.ds(b * tile, tile)
        pltpu.make_async_remote_copy(
            src_ref=feat_v.at[slot, :, span],
            dst_ref=mid_v.at[slot, :, span],
            send_sem=fsend_sem.at[0, b],
            recv_sem=frecv_sem.at[slot, b],
            device_id=dev(grp, win, slot),
            device_id_type=MESH,
        ).wait_recv()

    behind = {}

    def feature_forward(b):
        span = pl.ds(b * tile, tile)
        behind[b] = []
        for i in range(half):
            at = (seq + i) % half
            if i == 0:

                @pl.when(seq < half)
                def _():
                    feature_wait(half + at, b)

            else:
                feature_wait(half + at, b)
            behind[b].append(
                pltpu.make_async_remote_copy(
                    src_ref=mid_v.at[half + at, :, span],
                    dst_ref=got_v.at[at, :, span],
                    send_sem=bsend_sem.at[i, b],
                    recv_sem=brecv_sem.at[i, b],
                    device_id=dev(grp, next_win, seq),
                    device_id_type=MESH,
                )
            )
            behind[b][i].start()

    paired = {}

    def blend(b):
        for i in range(half):
            at = (seq + i) % half
            if i == 0:

                @pl.when(seq >= half)
                def _():
                    feature_wait(at, b)

            else:
                feature_wait(at, b)
        for copy in behind[b]:
            copy.wait_recv()
        for m in range(tile // 128):
            at = slice(b * tile + m * 128, b * tile + (m + 1) * 128)
            blocks = []
            for i in range(half):
                offset = lax.broadcasted_iota(jnp.int32, (piece, 128), 0) + (i * n + seq) * piece
                offset = offset.astype(jnp.float32)
                blocks.append(
                    (
                        (offset + 1.0) * mid_v[i, :, at].astype(jnp.float32)
                        + (window_len - offset) * got_v[i, :, at].astype(jnp.float32)
                    )
                    * (1.0 / (window_len + 1.0))
                )
            blend_v[0, :, at] = jnp.concatenate(blocks, axis=0).astype(jnp.bfloat16)
        span = pl.ds(b * tile, tile)
        paired[b] = remote(blend_v.at[0, :, span], blend_v.at[1, :, span], sibling)

    step = min(cols, HEAD_TILE)
    steps = cols // step

    def head_product(lo, hi, who, h, t):
        at = pl.ds(pl.multiple_of(t * step, step), step)
        span = slice(lo * tile, hi * tile)
        return jnp.dot(blend_v[who, :, span], wh_v[h, span, at], preferred_element_type=jnp.float32)

    def head_add(lo, hi, who):
        for b in range(lo, hi):
            if who == 0:
                head_ready(b)
            else:
                paired[b].wait_recv()

        def body(k, carry):
            h, t = k // steps, k % steps
            at = pl.ds(pl.multiple_of(k * step, step), step)
            part = head_product(lo, hi, who, h, t)
            acc_v[who, :, at] = part if lo == 0 else acc_v[who, :, at] + part
            return carry

        lax.fori_loop(0, half * steps, body, 0)

    stores = []

    def head_last(lo, who, h):
        shard = 2 * h + core
        for t in range(steps):
            at = pl.ds(h * cols + t * step, step)
            base = pl.ds(pl.multiple_of(shard * cols + t * step, step), step)
            z = acc_v[who, :, at] + head_product(lo, BANDS, who, h, t) + bias_v[:, base]
            z = jnp.maximum(z, 0.0) + jnp.log1p(jnp.exp(-jnp.abs(z)))
            for i in range(half):
                out_v[who, i, :, at] = z[i * piece : (i + 1) * piece].astype(jnp.bfloat16)
            src = out_v.at[who, :, :, at]
            dst = out_h.at[:, :, base]
            if who == 0:
                stores.append(pltpu.make_async_copy(src, dst, store_sem.at[h, t]))
            else:
                stores.append(
                    pltpu.make_async_remote_copy(
                        src_ref=src,
                        dst_ref=dst,
                        send_sem=psend_sem.at[h, t],
                        recv_sem=precv_sem.at[h, t],
                        device_id=sibling,
                        device_id_type=MESH,
                    )
                )
            stores[-1].start()

    for c in range(EARLY):
        line_own(c)
    widen()
    for c in range(EARLY):
        line_step(c, 1)
    edge_queries()
    kv_relay(0)
    line_step(0, 2)
    attend(0)
    for c in range(1, EARLY):
        line_step(c, 2)
    for p in range(1, PAIRS):
        kv_relay(p)
        attend(p)
    loads["wo"].wait()
    loads["taps"].wait()
    line_step(0, 3)
    up_band(0)
    feature_out(0)
    head_spread(4)
    line_step(1, 3)
    up_band(1)
    feature_out(1)
    line_step(2, 3)
    up_band(2)
    feature_out(2)
    line_step(3, 3)
    up_band(3)
    feature_out(3)
    head_spread(5)
    up_band(4)
    feature_out(4)
    up_band(5)
    feature_out(5)
    loads["wh"].wait()
    loads["bias"].wait()
    feature_forward(0)
    head_relay(4)
    feature_forward(1)
    head_relay(5)
    feature_forward(2)
    feature_forward(3)
    blend(0)
    feature_forward(4)
    blend(1)
    feature_forward(5)
    blend(2)
    head_add(0, 3, 0)
    head_add(0, 3, 1)
    blend(3)
    head_add(3, 4, 0)
    blend(4)
    head_add(3, 4, 1)
    blend(5)
    for b in range(4, BANDS):
        head_ready(b)
    head_last(4, 0, 0)
    for b in range(4, BANDS):
        paired[b].wait_recv()
    for h in range(half):
        head_last(4, 1, h)
    for h in range(1, half):
        head_last(4, 0, h)

    for copy in stores:
        copy.wait()
    for copy in started:
        copy.wait_send()
    for cond, copy in maybe:

        @pl.when(cond)
        def _():
            copy.wait_send()

    for copy in feats:
        copy.wait_send()
    for copies in behind.values():
        for copy in copies:
            copy.wait_send()


def local(embeddings, skip_rows, w_query, w_key, w_value, w_out, conv_taps, w_head, head_bias):
    n = lax.axis_size("seq")
    n_win = lax.axis_size("win")
    n_grp = lax.axis_size("grp")
    _, tok, width = embeddings.shape
    cols = w_head.shape[1]
    piece = 2 * tok // n
    half = n // 2
    others = half - 1
    steps = cols // min(cols, HEAD_TILE)
    line = EARLY * (4 + 4 * (LINE - 1) - 2) + (BANDS - EARLY) * 4
    copies = PAIRS * (2 * others + 1) + line * others + BANDS + 4
    bf16, f32 = jnp.bfloat16, jnp.float32
    dma = pltpu.SemaphoreType.DMA
    tracks = pl.pallas_call(
        functools.partial(kernel, n, n_win, n_grp),
        out_shape=jax.ShapeDtypeStruct((half, piece, n * cols), bf16),
        in_specs=[pl.BlockSpec(memory_space=pl.ANY)] * 9,
        out_specs=pl.BlockSpec(memory_space=pl.ANY),
        scratch_shapes=[
            pltpu.VMEM((tok, width), bf16),
            pltpu.VMEM((2 * tok, width), bf16),
            pltpu.VMEM(w_query.shape, bf16),
            pltpu.VMEM(w_key.shape, bf16),
            pltpu.VMEM(w_value.shape, bf16),
            pltpu.VMEM(w_out.shape, bf16),
            pltpu.VMEM(conv_taps.shape, f32),
            pltpu.VMEM((1, n * cols), f32),
            pltpu.VMEM((half, width, cols), bf16),
            pltpu.VMEM((2, 8, width), bf16),
            pltpu.VMEM((2, 8, width), bf16),
            pltpu.VMEM((tok + 16, HEADS * KEY), bf16),
            pltpu.VMEM((n, PAIRS, tok, KP + VP), bf16),
            pltpu.VMEM((tok + 16, HEADS * VAL), bf16),
            pltpu.VMEM((width // 128, 2 * tok, 128), f32),
            pltpu.VMEM((width // BANDS // 128, tok, 128), f32),
            pltpu.VMEM((width // BANDS // 128, tok, 128), f32),
            pltpu.VMEM((n, piece, width), bf16),
            pltpu.VMEM((n, piece, width), bf16),
            pltpu.VMEM((half, piece, width), bf16),
            pltpu.VMEM((2, tok, width), bf16),
            pltpu.VMEM((2, tok, half * cols), f32),
            pltpu.VMEM((2, half, piece, half * cols), bf16),
            dma((9,)),
            dma((copies,)),
            dma((copies,)),
            dma((n, BANDS)),
            dma((n, BANDS)),
            dma((half, BANDS)),
            dma((half, BANDS)),
            dma((half, steps)),
            dma((half, steps)),
            dma((half, steps)),
        ],
        compiler_params=pltpu.CompilerParams(
            collective_id=0, has_side_effects=True, vmem_limit_bytes=60 * 1024 * 1024
        ),
    )(
        embeddings, skip_rows, w_query, w_key, w_value, w_out, conv_taps, w_head,
        head_bias.reshape(1, -1),
    )
    return tracks[None, :, None]


def solution(mesh):
    return jax.shard_map(
        local,
        mesh=mesh,
        in_specs=(
            P(("grp", "win"), "seq", None),
            P(("grp", "win"), "seq", None),
            P(),
            P(),
            P(),
            P(),
            P(),
            P(None, "seq"),
            P(),
        ),
        out_specs=P(("grp", "win"), None, "seq", None, None),
        check_vma=False,
    )
```

```python
import functools
import math

import jax
import jax.numpy as jnp
from jax import lax
from jax.experimental import pallas as pl
from jax.experimental.pallas import tpu as pltpu
from jax.sharding import PartitionSpec as P

HEADS = 4
KEY = 64
VAL = 192
PAIRS = HEADS // 2
KP = 2 * KEY
VP = 2 * VAL
BANDS = 6
HEAD_TILE = 512
EARLY = 4
LINE = 4
MESH = pl.DeviceIdType.MESH


def normalize(rows):
    centre = jnp.mean(rows, axis=-1, keepdims=True)
    centred = rows - centre
    spread = jnp.mean(centred * centred, axis=-1, keepdims=True)
    return centred * lax.rsqrt(spread + 1e-05)


def gelu(x):
    return 0.5 * x * (1.0 + lax.erf(x * math.sqrt(0.5)))


def kernel(
    n, n_win, n_grp,
    emb_h, skip_h, wq_h, wk_h, wv_h, wo_h, taps_h, wh_h, bias_h, out_h,
    x_v, skip_v, wq_v, wk_v, wv_v, wo_v, taps_v, bias_v, wh_v,
    xh_v, sh_v, q_v, kv_v, att_v, wide_v, even_v, odd_v,
    feat_v, mid_v, got_v, blend_v, acc_v, out_v,
    load_sem, send_sem, recv_sem, fsend_sem, frecv_sem, bsend_sem, brecv_sem,
    store_sem, psend_sem, precv_sem,
):
    grp = lax.axis_index("grp")
    win = lax.axis_index("win")
    seq = lax.axis_index("seq")
    tok, width = x_v.shape
    piece = feat_v.shape[1]
    cols = wh_v.shape[2]
    half = n // 2
    tile = width // BANDS
    window_len = n * tok
    core = seq % 2
    row = seq // 2

    def dev(g, w, s):
        return (g, w, s)

    sibling = dev(grp, win, seq + 1 - 2 * core)
    other_grp = 1 - grp
    other_win = win + 1 - 2 * (win % 2)
    across = dev(other_grp, win, seq)
    beside = dev(grp, other_win, seq)
    peers = [(seq + 2 * e) % n for e in range(1, half)]
    next_win = (win + 1) % n_win
    prev_win = (win + n_win - 1) % n_win

    barrier = pltpu.get_barrier_semaphore()
    greeted = [dev(grp, win, (seq + d) % n) for d in range(1, n)]
    greeted += [dev(grp, w, seq) for w in (next_win, prev_win)]
    greeted.append(across)
    for target in greeted:
        pl.semaphore_signal(barrier, inc=1, device_id=target, device_id_type=MESH)

    loads = {}
    local_copies = {
        "x": (emb_h.at[0], x_v),
        "wk": (wk_h, wk_v),
        "wv": (wv_h, wv_v),
        "wq": (wq_h, wq_v),
        "skip": (skip_h.at[0], skip_v),
        "wo": (wo_h, wo_v),
        "taps": (taps_h, taps_v),
        "bias": (bias_h, bias_v),
        "wh": (wh_h, wh_v.at[row]),
    }

    def load(*names):
        for name in names:
            loads[name] = pltpu.make_async_copy(*local_copies[name], load_sem.at[len(loads)])
            loads[name].start()

    load("x", "wk", "wv")
    pl.semaphore_wait(barrier, len(greeted))

    started, maybe = [], []

    def remote(src, dst, target):
        at = len(started) + len(maybe)
        copy = pltpu.make_async_remote_copy(
            src_ref=src,
            dst_ref=dst,
            send_sem=send_sem.at[at],
            recv_sem=recv_sem.at[at],
            device_id=target,
            device_id_type=MESH,
        )
        copy.start()
        started.append(copy)
        return copy

    place = win % LINE
    left = dev(grp, prev_win, seq)
    right = dev(grp, next_win, seq)
    def remote_if(cond, src, dst, target):
        at = len(started) + len(maybe)
        copy = pltpu.make_async_remote_copy(
            src_ref=src,
            dst_ref=dst,
            send_sem=send_sem.at[at],
            recv_sem=recv_sem.at[at],
            device_id=target,
            device_id_type=MESH,
        )

        @pl.when(cond)
        def _():
            copy.start()

        maybe.append((cond, copy))
        return copy

    def rows_of(g, w, c):
        if c < EARLY:
            part = tile // (LINE * n_grp)
            first = c * tile + (g * LINE + w % LINE) * part
        else:
            part = tile // (2 * n_grp)
            first = c * tile + (g * 2 + w % 2) * part
        return pl.ds(pl.multiple_of(first, part), part)

    arrived = set()

    def arrive(copy):
        if id(copy) not in arrived:
            arrived.add(id(copy))
            copy.wait_recv()

    far = [(row + half - e) % half for e in range(1, half)]
    y_in, x_in, z_in, diag_in = {}, {}, {}, {}

    def head_out(c):
        rows = rows_of(grp, win, c)
        y_in[c] = [remote(wh_h.at[rows], wh_v.at[row, rows], dev(grp, win, p)) for p in peers]

    moving, crossing = {}, {}

    def line_own(c):
        rows = rows_of(grp, win, c)
        x_in[c], moving[c], crossing[c] = [], {}, []
        for e, at in enumerate(far):
            arrive(y_in[c][e])
            block = wh_v.at[at, rows]
            moving[c][1, e, 0] = remote_if(place < LINE - 1, block, block, right)
            moving[c][1, e, 1] = remote_if(place > 0, block, block, left)
            x_in[c].append(remote(block, block, across))

    def line_step(c, s):
        for e, at in enumerate(far):
            for way in range(2):
                has = place >= s if way == 0 else place + s < LINE
                goes = place < LINE - 1 if way == 0 else place > 0
                came = moving[c][s, e, way]

                @pl.when(has)
                def _():
                    came.wait_recv()

                rows = rows_of(grp, place - s if way == 0 else place + s, c)
                block = wh_v.at[at, rows]
                if s < LINE - 1:
                    moving[c][s + 1, e, way] = remote_if(
                        jnp.logical_and(has, goes), block, block, right if way == 0 else left
                    )
                crossing[c].append((has, remote_if(has, block, block, across)))

    def head_spread(c):
        rows = rows_of(grp, win, c)
        x_in[c], z_in[c] = [], []
        for copy, at in zip(y_in[c], far):
            arrive(copy)
            block = wh_v.at[at, rows]
            z_in[c].append(remote(block, block, beside))
            x_in[c].append(remote(block, block, across))

    def head_relay(c):
        diag_in[c] = []
        for copy, at in zip(z_in[c], far):
            arrive(copy)
            block = wh_v.at[at, rows_of(grp, other_win, c)]
            diag_in[c].append(remote(block, block, across))

    def head_ready(c):
        if c < EARLY:
            for copy in x_in[c]:
                arrive(copy)
            for has, copy in crossing[c]:

                @pl.when(has)
                def _():
                    copy.wait_recv()

        else:
            for copies in (y_in, x_in, z_in, diag_in):
                for copy in copies[c]:
                    arrive(copy)

    next_seq = dev(grp, win, (seq + 1) % n)
    prev_seq = dev(grp, win, (seq + n - 1) % n)
    for c in range(EARLY):
        head_out(c)
    edges = [
        remote(emb_h.at[0, pl.ds(tok - 8, 8)], xh_v.at[0], next_seq),
        remote(emb_h.at[0, pl.ds(0, 8)], xh_v.at[1], prev_seq),
        remote(skip_h.at[0, pl.ds(2 * tok - 8, 8)], sh_v.at[0], next_seq),
        remote(skip_h.at[0, pl.ds(0, 8)], sh_v.at[1], prev_seq),
    ]
    load("wq")

    loads["x"].wait()
    normed = normalize(x_v[...].astype(jnp.float32)).astype(jnp.bfloat16)
    loads["wk"].wait()
    loads["wv"].wait()
    kv_far, kv_near = [], []
    for p in range(PAIRS):
        kv_v[seq, p, :, :KP] = jnp.dot(
            normed, wk_v[:, p * KP : (p + 1) * KP], preferred_element_type=jnp.float32
        ).astype(jnp.bfloat16)
        kv_v[seq, p, :, KP:] = jnp.dot(
            normed, wv_v[:, p * VP : (p + 1) * VP], preferred_element_type=jnp.float32
        ).astype(jnp.bfloat16)
        block = kv_v.at[seq, p]
        kv_far.append([remote(block, block, dev(grp, win, s)) for s in peers])
        kv_near.append([remote(block, block, sibling)])
    for c in range(EARLY, BANDS):
        head_out(c)
    load("skip", "wo", "taps", "bias", "wh")
    loads["wq"].wait()
    q_v[:tok] = jnp.dot(normed, wq_v[...], preferred_element_type=jnp.float32).astype(jnp.bfloat16)
    def edge_queries():
        for copy in edges:
            copy.wait_recv()
        edge_x = jnp.concatenate([xh_v[0].astype(jnp.float32), xh_v[1].astype(jnp.float32)], axis=0)
        q_v[tok:] = jnp.dot(
            normalize(edge_x).astype(jnp.bfloat16), wq_v[...], preferred_element_type=jnp.float32
        ).astype(jnp.bfloat16)

    def widen():
        loads["skip"].wait()
        for j in range(width // 128):
            wide_v[j] = skip_v[:, j * 128 : (j + 1) * 128].astype(jnp.float32)

    def kv_relay(p):
        for e in range(half - 1):
            kv_far[p][e].wait_recv()
            block = kv_v.at[(seq + n - 2 * (e + 1)) % n, p]
            kv_near[p].append(remote(block, block, sibling))

    def attend(p):
        for copy in kv_near[p]:
            copy.wait_recv()
        keys = kv_v[:, p, :, :KP].reshape(n * tok, KP)
        vals = kv_v[:, p, :, KP:].reshape(n * tok, VP)
        pair = q_v[:, p * KP : (p + 1) * KP]
        key_lane = lax.broadcasted_iota(jnp.int32, pair.shape, 1)
        outs = []
        for h in range(2):
            mine = key_lane < KEY if h == 0 else key_lane >= KEY
            masked = jnp.where(mine, pair.astype(jnp.float32), 0.0).astype(jnp.bfloat16)
            scores = lax.dot_general(
                masked, keys, (((1,), (1,)), ((), ())), preferred_element_type=jnp.float32
            ) * (1.0 / math.sqrt(KEY))
            expo = jnp.exp(scores - jnp.max(scores, axis=-1, keepdims=True))
            denom = jnp.sum(expo, axis=-1, keepdims=True)
            outs.append(
                jnp.dot(expo.astype(jnp.bfloat16), vals, preferred_element_type=jnp.float32) / denom
            )
        val_lane = lax.broadcasted_iota(jnp.int32, outs[0].shape, 1)
        att_v[:, p * VP : (p + 1) * VP] = jnp.where(val_lane < VAL, outs[0], outs[1]).astype(
            jnp.bfloat16
        )

    def up_band(b):
        at = slice(b * tile, (b + 1) * tile)
        mixed = jnp.dot(att_v[...], wo_v[:, at], preferred_element_type=jnp.float32)
        resid = x_v[:, at].astype(jnp.float32) + mixed[:tok]
        first = xh_v[0, :, at].astype(jnp.float32) + mixed[tok : tok + 8]
        last = xh_v[1, :, at].astype(jnp.float32) + mixed[tok + 8 :]
        first = (first[7:8] + sh_v[0, :, at].astype(jnp.float32)[7:8]).astype(jnp.bfloat16)
        last = (last[0:1] + sh_v[1, :, at].astype(jnp.float32)[0:1]).astype(jnp.bfloat16)
        before = jnp.where(seq == 0, 0.0, first.astype(jnp.float32))
        after = jnp.where(seq == n - 1, 0.0, last.astype(jnp.float32))
        for m in range(tile // 128):
            j = b * (tile // 128) + m
            mine = resid[:, m * 128 : (m + 1) * 128]
            even_v[m] = (
                (mine + wide_v[j, pl.ds(0, tok, stride=2), :]).astype(jnp.bfloat16).astype(jnp.float32)
            )
            odd_v[m] = (
                (mine + wide_v[j, pl.ds(1, tok, stride=2), :]).astype(jnp.bfloat16).astype(jnp.float32)
            )
        for m in range(tile // 128):
            j = b * (tile // 128) + m
            here = slice(j * 128, (j + 1) * 128)
            lanes = slice(m * 128, (m + 1) * 128)
            even, odd = even_v[m], odd_v[m]
            line = lax.broadcasted_iota(jnp.int32, (tok, 128), 0)
            odd_prev = jnp.where(line == 0, before[:, lanes], pltpu.roll(odd, 1, axis=0))
            even_next = jnp.where(line == tok - 1, after[:, lanes], pltpu.roll(even, tok - 1, axis=0))
            t0, t1, t2 = taps_v[0:1, here], taps_v[1:2, here], taps_v[2:3, here]
            wide_v[j, pl.ds(0, tok, stride=2), :] = gelu(t0 * odd_prev + t1 * even + t2 * odd)
            wide_v[j, pl.ds(1, tok, stride=2), :] = gelu(t0 * even + t1 * odd + t2 * even_next)
            for k in range(n):
                feat_v[k, :, here] = wide_v[j, k * piece : (k + 1) * piece, :].astype(jnp.bfloat16)

    feats = []

    def feature_out(b):
        span = pl.ds(b * tile, tile)
        for d in list(range(half, n)) + list(range(1, half)):
            owner = (seq + d) % n
            feats.append(
                pltpu.make_async_remote_copy(
                    src_ref=feat_v.at[owner, :, span],
                    dst_ref=mid_v.at[seq, :, span],
                    send_sem=fsend_sem.at[d, b],
                    recv_sem=frecv_sem.at[seq, b],
                    device_id=dev(grp, win, owner),
                    device_id_type=MESH,
                )
            )
            feats[-1].start()
        mid_v[seq, :, span] = feat_v[seq, :, span]

    def feature_wait(slot, b):
        span = pl.ds(b * tile, tile)
        pltpu.make_async_remote_copy(
            src_ref=feat_v.at[slot, :, span],
            dst_ref=mid_v.at[slot, :, span],
            send_sem=fsend_sem.at[0, b],
            recv_sem=frecv_sem.at[slot, b],
            device_id=dev(grp, win, slot),
            device_id_type=MESH,
        ).wait_recv()

    behind = {}

    def feature_forward(b):
        span = pl.ds(b * tile, tile)
        behind[b] = []
        for i in range(half):
            at = (seq + i) % half
            if i == 0:

                @pl.when(seq < half)
                def _():
                    feature_wait(half + at, b)

            else:
                feature_wait(half + at, b)
            behind[b].append(
                pltpu.make_async_remote_copy(
                    src_ref=mid_v.at[half + at, :, span],
                    dst_ref=got_v.at[at, :, span],
                    send_sem=bsend_sem.at[i, b],
                    recv_sem=brecv_sem.at[i, b],
                    device_id=dev(grp, next_win, seq),
                    device_id_type=MESH,
                )
            )
            behind[b][i].start()

    paired = {}

    def blend(b):
        for i in range(half):
            at = (seq + i) % half
            if i == 0:

                @pl.when(seq >= half)
                def _():
                    feature_wait(at, b)

            else:
                feature_wait(at, b)
        for copy in behind[b]:
            copy.wait_recv()
        for m in range(tile // 128):
            at = slice(b * tile + m * 128, b * tile + (m + 1) * 128)
            blocks = []
            for i in range(half):
                offset = lax.broadcasted_iota(jnp.int32, (piece, 128), 0) + (i * n + seq) * piece
                offset = offset.astype(jnp.float32)
                blocks.append(
                    (
                        (offset + 1.0) * mid_v[i, :, at].astype(jnp.float32)
                        + (window_len - offset) * got_v[i, :, at].astype(jnp.float32)
                    )
                    * (1.0 / (window_len + 1.0))
                )
            blend_v[0, :, at] = jnp.concatenate(blocks, axis=0).astype(jnp.bfloat16)
        span = pl.ds(b * tile, tile)
        paired[b] = remote(blend_v.at[0, :, span], blend_v.at[1, :, span], sibling)

    step = min(cols, HEAD_TILE)
    steps = cols // step

    def head_product(lo, hi, who, h, t):
        at = pl.ds(pl.multiple_of(t * step, step), step)
        span = slice(lo * tile, hi * tile)
        return jnp.dot(blend_v[who, :, span], wh_v[h, span, at], preferred_element_type=jnp.float32)

    def head_add(lo, hi, who):
        for b in range(lo, hi):
            if who == 0:
                head_ready(b)
            else:
                paired[b].wait_recv()

        def body(k, carry):
            h, t = k // steps, k % steps
            at = pl.ds(pl.multiple_of(k * step, step), step)
            part = head_product(lo, hi, who, h, t)
            acc_v[who, :, at] = part if lo == 0 else acc_v[who, :, at] + part
            return carry

        lax.fori_loop(0, half * steps, body, 0)

    stores = []

    def head_last(lo, who, h):
        shard = 2 * h + core
        for t in range(steps):
            at = pl.ds(h * cols + t * step, step)
            base = pl.ds(pl.multiple_of(shard * cols + t * step, step), step)
            z = acc_v[who, :, at] + head_product(lo, BANDS, who, h, t) + bias_v[:, base]
            z = jnp.maximum(z, 0.0) + jnp.log1p(jnp.exp(-jnp.abs(z)))
            for i in range(half):
                out_v[who, i, :, at] = z[i * piece : (i + 1) * piece].astype(jnp.bfloat16)
            if who == 0:
                stores.append(
                    pltpu.make_async_copy(
                        out_v.at[0, :, :, at], out_h.at[:, :, base], store_sem.at[h, t]
                    )
                )
                stores[-1].start()
        if who == 1:
            whole = pl.ds(pl.multiple_of(shard * cols, cols), cols)
            stores.append(
                pltpu.make_async_remote_copy(
                    src_ref=out_v.at[1, :, :, pl.ds(h * cols, cols)],
                    dst_ref=out_h.at[:, :, whole],
                    send_sem=psend_sem.at[h],
                    recv_sem=precv_sem.at[h],
                    device_id=sibling,
                    device_id_type=MESH,
                )
            )
            stores[-1].start()

    for c in range(EARLY):
        line_own(c)
    widen()
    for c in range(EARLY):
        line_step(c, 1)
    edge_queries()
    kv_relay(0)
    line_step(0, 2)
    attend(0)
    for c in range(1, EARLY):
        line_step(c, 2)
    for p in range(1, PAIRS):
        kv_relay(p)
        attend(p)
    loads["wo"].wait()
    loads["taps"].wait()
    line_step(0, 3)
    up_band(0)
    feature_out(0)
    head_spread(4)
    line_step(1, 3)
    up_band(1)
    feature_out(1)
    line_step(2, 3)
    up_band(2)
    feature_out(2)
    line_step(3, 3)
    up_band(3)
    feature_out(3)
    head_spread(5)
    up_band(4)
    feature_out(4)
    up_band(5)
    feature_out(5)
    loads["wh"].wait()
    loads["bias"].wait()
    feature_forward(0)
    head_relay(4)
    feature_forward(1)
    head_relay(5)
    feature_forward(2)
    feature_forward(3)
    blend(0)
    feature_forward(4)
    blend(1)
    feature_forward(5)
    blend(2)
    head_add(0, 3, 0)
    head_add(0, 3, 1)
    blend(3)
    head_add(3, 4, 0)
    blend(4)
    head_add(3, 4, 1)
    blend(5)
    for b in range(4, BANDS):
        head_ready(b)
    head_last(4, 0, 0)
    for b in range(4, BANDS):
        paired[b].wait_recv()
    for h in range(half):
        head_last(4, 1, h)
    for h in range(1, half):
        head_last(4, 0, h)

    for copy in stores:
        copy.wait()
    for copy in started:
        copy.wait_send()
    for cond, copy in maybe:

        @pl.when(cond)
        def _():
            copy.wait_send()

    for copy in feats:
        copy.wait_send()
    for copies in behind.values():
        for copy in copies:
            copy.wait_send()


def local(embeddings, skip_rows, w_query, w_key, w_value, w_out, conv_taps, w_head, head_bias):
    n = lax.axis_size("seq")
    n_win = lax.axis_size("win")
    n_grp = lax.axis_size("grp")
    _, tok, width = embeddings.shape
    cols = w_head.shape[1]
    piece = 2 * tok // n
    half = n // 2
    others = half - 1
    steps = cols // min(cols, HEAD_TILE)
    line = EARLY * (4 + 4 * (LINE - 1) - 2) + (BANDS - EARLY) * 4
    copies = PAIRS * (2 * others + 1) + line * others + BANDS + 4
    bf16, f32 = jnp.bfloat16, jnp.float32
    dma = pltpu.SemaphoreType.DMA
    tracks = pl.pallas_call(
        functools.partial(kernel, n, n_win, n_grp),
        out_shape=jax.ShapeDtypeStruct((half, piece, n * cols), bf16),
        in_specs=[pl.BlockSpec(memory_space=pl.ANY)] * 9,
        out_specs=pl.BlockSpec(memory_space=pl.ANY),
        scratch_shapes=[
            pltpu.VMEM((tok, width), bf16),
            pltpu.VMEM((2 * tok, width), bf16),
            pltpu.VMEM(w_query.shape, bf16),
            pltpu.VMEM(w_key.shape, bf16),
            pltpu.VMEM(w_value.shape, bf16),
            pltpu.VMEM(w_out.shape, bf16),
            pltpu.VMEM(conv_taps.shape, f32),
            pltpu.VMEM((1, n * cols), f32),
            pltpu.VMEM((half, width, cols), bf16),
            pltpu.VMEM((2, 8, width), bf16),
            pltpu.VMEM((2, 8, width), bf16),
            pltpu.VMEM((tok + 16, HEADS * KEY), bf16),
            pltpu.VMEM((n, PAIRS, tok, KP + VP), bf16),
            pltpu.VMEM((tok + 16, HEADS * VAL), bf16),
            pltpu.VMEM((width // 128, 2 * tok, 128), f32),
            pltpu.VMEM((width // BANDS // 128, tok, 128), f32),
            pltpu.VMEM((width // BANDS // 128, tok, 128), f32),
            pltpu.VMEM((n, piece, width), bf16),
            pltpu.VMEM((n, piece, width), bf16),
            pltpu.VMEM((half, piece, width), bf16),
            pltpu.VMEM((2, tok, width), bf16),
            pltpu.VMEM((2, tok, half * cols), f32),
            pltpu.VMEM((2, half, piece, half * cols), bf16),
            dma((9,)),
            dma((copies,)),
            dma((copies,)),
            dma((n, BANDS)),
            dma((n, BANDS)),
            dma((half, BANDS)),
            dma((half, BANDS)),
            dma((half, steps)),
            dma((half,)),
            dma((half,)),
        ],
        compiler_params=pltpu.CompilerParams(
            collective_id=0, has_side_effects=True, vmem_limit_bytes=60 * 1024 * 1024
        ),
    )(
        embeddings, skip_rows, w_query, w_key, w_value, w_out, conv_taps, w_head,
        head_bias.reshape(1, -1),
    )
    return tracks[None, :, None]


def solution(mesh):
    return jax.shard_map(
        local,
        mesh=mesh,
        in_specs=(
            P(("grp", "win"), "seq", None),
            P(("grp", "win"), "seq", None),
            P(),
            P(),
            P(),
            P(),
            P(),
            P(None, "seq"),
            P(),
        ),
        out_specs=P(("grp", "win"), None, "seq", None, None),
        check_vma=False,
    )
```
